256 devices in a mesh: row: 16 (over z, core), col: 16 (over x, y).
Axes of the slice: x: 4, y: 4, z: 8, core: 2. Of those that a mesh axis runs over, the one named last changes fastest.
Arguments:
- gram: float32 [16, 16, 1024, 1024], P('row', 'col'), may hold values from -21834.348 to 21835.348, as said below
Outputs:
- factored: float32 [16, 16, 1024, 1024], P('row', 'col')
The draws below stay inside these ranges and needn't reach their ends.
Inputs may be any that keep to these rules, and one draw needn't show every extreme that they name: gram holds a symmetric positive definite matrix of order 16384 whose smallest eigenvalue is at least 1.
All inputs are finite; a program needn't handle non-finite values.
Results may differ from the reference program's by a relative error of at most 0.0001.
Values sent between devices are 32-bit elements; how exact they have to be, the bound alone decides.
No kernel may reach another device: no remote copies, remote signals or barrier semaphores. Data moves between devices by JAX's collectives and lax.ppermute only.
A program may use at most 64 MiB of HBM per device.

```python
import math
import jax
import jax.numpy as jnp
from jax import lax

BS = 256
PANELS = 3
ORDER = 16384
RBLK = 4
CBLK = 4
N_ROW = 16
N_COL = 16


def draw_gram(key, part):
    first_key = jax.random.fold_in(jax.random.fold_in(key, 17), 0)
    inner = ORDER // 4
    window = BS // 2
    noise = jax.random.truncated_normal(first_key, -6.0, 6.0, (ORDER, inner), jnp.float32)
    padded = jnp.concatenate([jnp.zeros((window, inner), jnp.float32), noise], axis=0)
    running = jnp.concatenate([jnp.zeros((1, inner), jnp.float32), jnp.cumsum(padded, axis=0)], axis=0)
    recent = (running[window:window + ORDER] - running[0:ORDER]) / math.sqrt(window)
    factor = noise + recent
    product = jnp.dot(factor, factor.T, precision=lax.Precision.HIGHEST, preferred_element_type=jnp.float32)
    symmetric = product / inner + jnp.eye(ORDER, dtype=jnp.float32)
    return symmetric.reshape(RBLK, N_ROW, BS, CBLK, N_COL, BS).transpose(1, 4, 0, 2, 3, 5).reshape(N_ROW, N_COL, RBLK * BS, CBLK * BS)


def setup_inputs(seed: int = 0) -> dict:
    seeds = jax.random.split(jax.random.key(seed), 2)
    return {
        "gram": draw_gram(jax.random.fold_in(seeds[1], 71), 0),
    }


def reference(gram):
    matrix = gram.reshape(N_ROW, N_COL, RBLK, BS, CBLK, BS).transpose(2, 0, 3, 4, 1, 5).reshape(ORDER, ORDER)
    for panel_step in range(PANELS):
        start = panel_step * BS
        stop = start + BS
        diagonal = jnp.linalg.cholesky(matrix[start:stop, start:stop])
        below = matrix[stop:, start:stop]
        panel = lax.linalg.triangular_solve(diagonal, below, left_side=False, lower=True, transpose_a=True)
        update = jnp.dot(panel.astype(jnp.float32), panel.T.astype(jnp.float32), precision=lax.Precision.HIGHEST, preferred_element_type=jnp.float32)
        matrix = matrix.at[stop:, stop:].set(matrix[stop:, stop:] - update)
        matrix = matrix.at[start:stop, start:stop].set(diagonal)
        matrix = matrix.at[stop:, start:stop].set(panel)
        matrix = matrix.at[start:stop, stop:].set(jnp.zeros((BS, ORDER - stop), jnp.float32))
    return matrix.reshape(RBLK, N_ROW, BS, CBLK, N_COL, BS).transpose(1, 4, 0, 2, 3, 5).reshape(N_ROW, N_COL, RBLK * BS, CBLK * BS)
```

```python
import jax
import jax.numpy as jnp
from jax import lax
from jax.experimental import pallas as pl
from jax.experimental.pallas import tpu as pltpu
from jax.sharding import Mesh
from jax.sharding import PartitionSpec as P

BS = 256
PANELS = 3
WIDTH = PANELS * BS
FACTOR = 128
ROW = ("row_0", "row_1")
COL = ("col_0", "col_1")
FULL = lax.Precision.HIGHEST
UPPER = ((0, 0), (0, 1), (0, 2), (1, 1), (1, 2), (2, 2))


def full_dot(left, right, dims):
    return lax.dot_general(
        left, right, (dims, ((), ())), precision=FULL, preferred_element_type=jnp.float32
    )


def factor_inverse(block):
    tiles = [block[8 * b : 8 * b + 8] for b in range(FACTOR // 8)]
    lane = lax.broadcasted_iota(jnp.int32, (8, FACTOR), 1)
    sub = lax.broadcasted_iota(jnp.int32, (8, FACTOR), 0)
    for k in range(FACTOR):
        first, s = divmod(k, 8)
        pivot = tiles[first][s : s + 1]
        scaled = jnp.where(lane[:1] == k, 1.0, pivot) * (1.0 / pivot[:, k : k + 1])
        for b in range(first, FACTOR // 8):
            tile = tiles[b]
            new = jnp.where(lane == k, 0.0, tile) - tile[:, k : k + 1] * scaled
            tiles[b] = jnp.where(sub > s, new, tile) if b == first else new
    rows = []
    for b, tile in enumerate(tiles):
        own = lane == sub + 8 * b
        pivots = jnp.sum(jnp.where(own, tile, 0.0), axis=1, keepdims=True)
        scale = lax.rsqrt(pivots)
        scale = scale * (1.5 - 0.5 * pivots * scale * scale)
        rows.append(jnp.where(lane < sub + 8 * b, tile * scale, jnp.where(own, scale, 0.0)))
    return jnp.concatenate(rows, axis=0)


def corner_kernel(corner, inverse, work):
    work[...] = jnp.zeros((WIDTH, WIDTH), jnp.float32)
    for n, (i, j) in enumerate(UPPER):
        work[i * BS : i * BS + BS, j * BS : j * BS + BS] = corner[:, n].reshape(BS, BS)
    for low in range(0, WIDTH, FACTOR):
        high = low + FACTOR
        own = factor_inverse(work[low:high, low:high])
        rows = full_dot(own, work[low:high, :], ((1,), (0,)))
        left = jnp.concatenate([rows[:, :low], own], axis=1) if low else own
        if high == WIDTH:
            inverse[low:high, :] = left
            break
        right = rows[:, high:]
        inverse[low:high, :] = jnp.concatenate([left, jnp.zeros_like(right)], axis=1)
        change = full_dot(right, jnp.concatenate([left, right], axis=1), ((0,), (0,)))
        if low:
            work[high:, :low] = work[high:, :low] - change[:, :low]
        work[high:, low:high] = -change[:, low:high]
        work[high:, high:] = work[high:, high:] - change[:, high:]


def corner_inverse(corner):
    return pl.pallas_call(
        corner_kernel,
        out_shape=jax.ShapeDtypeStruct((WIDTH, WIDTH), jnp.float32),
        scratch_shapes=[pltpu.VMEM((WIDTH, WIDTH), jnp.float32)],
        compiler_params=pltpu.CompilerParams(vmem_limit_bytes=56 << 20),
        name="corner",
    )(corner)


def solved(lines, inverse, store):
    for k in range(PANELS):
        total = None
        for j in range(k + 1):
            part = full_dot(lines[j], inverse[k * BS : k * BS + BS, j * BS : j * BS + BS], ((1,), (1,)))
            total = part if total is None else total + part
        store(k, total)


def panel_kernel(place, rows, cols, inverse, matrix, out, right, left):
    i = pl.program_id(0)
    own_row, own_col = place[0], place[1]
    count = matrix.shape[1] // BS

    @pl.when(i == 0)
    def _():
        for c in range(count):
            lines = [cols[4 * c : 4 * c + 4, k].reshape(BS, BS) for k in range(PANELS)]

            def keep(k, value, c=c):
                right[c * BS : c * BS + BS, k * BS : k * BS + BS] = value

            solved(lines, inverse, keep)

    def keep_left(k, value):
        left[:, k * BS : k * BS + BS] = value

    solved([rows[:, k].reshape(BS, BS) for k in range(PANELS)], inverse, keep_left)
    out[...] = matrix[...] - full_dot(left[...], right[...], ((1,), (1,)))
    block_row = i * 16 + own_row

    @pl.when(block_row < PANELS)
    def _():
        out[...] = jnp.zeros(out.shape, jnp.float32)

    for k in range(PANELS):

        @pl.when(own_col == k)
        def _(k=k):
            panel = left[:, k * BS : k * BS + BS]
            r = lax.broadcasted_iota(jnp.int32, (BS, BS), 0) + block_row * BS
            s = lax.broadcasted_iota(jnp.int32, (BS, BS), 1) + k * BS
            out[:, :BS] = jnp.where(r >= s, panel, 0.0)


def panel_update(place, rows, cols, inverse, matrix):
    size = matrix.shape[0]
    steps = size // BS
    pieces = rows.shape[0] // steps
    return pl.pallas_call(
        panel_kernel,
        grid_spec=pltpu.PrefetchScalarGridSpec(
            num_scalar_prefetch=1,
            grid=(steps,),
            in_specs=[
                pl.BlockSpec((pieces,) + rows.shape[1:], lambda i, _: (i, 0, 0, 0)),
                pl.BlockSpec(cols.shape, lambda i, _: (0, 0, 0, 0)),
                pl.BlockSpec(inverse.shape, lambda i, _: (0, 0)),
                pl.BlockSpec((BS, size), lambda i, _: (i, 0)),
            ],
            out_specs=pl.BlockSpec((BS, size), lambda i, _: (i, 0)),
            scratch_shapes=[
                pltpu.VMEM((size, WIDTH), jnp.float32),
                pltpu.VMEM((BS, WIDTH), jnp.float32),
            ],
        ),
        out_shape=jax.ShapeDtypeStruct(matrix.shape, jnp.float32),
        compiler_params=pltpu.CompilerParams(vmem_limit_bytes=56 << 20),
        name="panels",
    )(place, rows, cols, inverse, matrix)


def gathered(piece, axes):
    copies = jnp.broadcast_to(piece[None], (16,) + piece.shape)
    return lax.all_to_all(copies, axes, 0, 0, tiled=True)


def down_rows(piece):
    z = lax.axis_index("row_0")
    core = lax.axis_index("row_1")
    other = lax.ppermute(piece, "row_1", [(0, 1), (1, 0)])
    even = jnp.where(core == 0, piece, other)
    odd = jnp.where(core == 0, other, piece)
    met = lax.ppermute((even, odd), "row_0", [(0, 1), (1, 0)])
    near = z < 2
    first = jnp.where(z == 0, even, met[0])
    second = jnp.where(z == 0, odd, met[1])
    third = jnp.where(z == 0, met[0], even)
    have = jnp.stack([first, second, third])
    got = lax.ppermute(have, "row_0", [(0, 7), (1, 2)])
    have = jnp.where(near, have, got)
    got = lax.ppermute(have, "row_0", [(0, 6), (7, 5), (1, 3), (2, 4)])
    return jnp.where((z < 3) | (z == 7), have, got)


def on_device(gram):
    matrix = gram[0, 0]
    own_row = lax.axis_index(ROW)
    own_col = lax.axis_index(COL)
    place = jnp.stack([own_row, own_col]).astype(jnp.int32)
    top = matrix[:BS, :BS].reshape(16, 16, BS)
    top = lax.all_to_all(top, COL, 0, 0, tiled=True)[:PANELS]
    side = matrix[:, :BS].reshape(16, 64, BS)
    side = lax.all_to_all(side, COL, 0, 0, tiled=True)[:PANELS]
    lines = down_rows(top)
    corner = gathered(jnp.stack([lines[i, j] for i, j in UPPER]), COL)
    turned = lax.ppermute(side, ROW + COL, [(p * 16 + j, j * 16 + p) for p in range(16) for j in range(16)])
    rows = gathered(side, COL)
    cols = lax.all_gather(turned, ROW)
    inverse = corner_inverse(corner)
    return panel_update(place, rows, cols, inverse, matrix)[None, None]


def solution(mesh):
    split = Mesh(mesh.devices.reshape(8, 2, 4, 4), ROW + COL)
    return jax.shard_map(
        on_device,
        mesh=split,
        in_specs=(P(ROW, COL, None, None),),
        out_specs=P(ROW, COL, None, None),
        check_vma=False,
    )
```

```python
import jax
import jax.numpy as jnp
from jax import lax
from jax.experimental import pallas as pl
from jax.experimental.pallas import tpu as pltpu
from jax.sharding import Mesh
from jax.sharding import PartitionSpec as P

BS = 256
PANELS = 3
WIDTH = PANELS * BS
FACTOR = 128
ROW = ("row_0", "row_1")
COL = ("col_0", "col_1")
FULL = lax.Precision.HIGHEST
UPPER = ((0, 0), (0, 1), (0, 2), (1, 1), (1, 2), (2, 2))


def full_dot(left, right, dims):
    return lax.dot_general(
        left, right, (dims, ((), ())), precision=FULL, preferred_element_type=jnp.float32
    )


def wide(line):
    return jnp.broadcast_to(line, (8, FACTOR))


def factor_inverse(block):
    count = FACTOR // 8
    tiles = [block[8 * b : 8 * b + 8] for b in range(count)]
    lane = lax.broadcasted_iota(jnp.int32, (8, FACTOR), 1)
    sub = lax.broadcasted_iota(jnp.int32, (8, FACTOR), 0)
    for b in range(count):
        cols = {t: [wide(tiles[t][:, 8 * b + j : 8 * b + j + 1]) for j in range(8)] for t in range(b, count)}
        for s in range(8):
            at = lane == 8 * b + s
            own = cols[b]
            inv = 1.0 / wide(own[s][s : s + 1])
            heads = [wide(own[j][s : s + 1]) for j in range(8)]
            pivot = jnp.where(at, 1.0, wide(tiles[b][s : s + 1]))
            for t in range(b, count):
                scale = cols[t][s] * inv
                rest = jnp.where(at, 0.0, tiles[t])
                if t == b:
                    scale = jnp.where(sub > s, scale, 0.0)
                    rest = jnp.where(sub > s, rest, tiles[t])
                for j in range(s + 1, 8):
                    cols[t][j] = cols[t][j] - scale * heads[j]
                tiles[t] = rest - scale * pivot
    rows = []
    for b, tile in enumerate(tiles):
        own = lane == sub + 8 * b
        pivots = jnp.sum(jnp.where(own, tile, 0.0), axis=1, keepdims=True)
        scale = lax.rsqrt(pivots)
        scale = scale * (1.5 - 0.5 * pivots * scale * scale)
        rows.append(jnp.where(lane < sub + 8 * b, tile * scale, jnp.where(own, scale, 0.0)))
    return jnp.concatenate(rows, axis=0)


def eliminate(work, inverse, lows):
    for low in lows:
        high = low + FACTOR
        own = factor_inverse(work[low:high, low:high])
        rows = full_dot(own, work[low:high, :], ((1,), (0,)))
        left = jnp.concatenate([rows[:, :low], own], axis=1) if low else own
        if high == WIDTH:
            inverse[low:high, :] = left
            break
        right = rows[:, high:]
        inverse[low:high, :] = jnp.concatenate([left, jnp.zeros_like(right)], axis=1)
        change = full_dot(right, jnp.concatenate([left, right], axis=1), ((0,), (0,)))
        if low:
            work[high:, :low] = work[high:, :low] - change[:, :low]
        work[high:, low:high] = -change[:, low:high]
        work[high:, high:] = work[high:, high:] - change[:, high:]


def corner_first(place, mine, other, inverse, work):
    work[...] = jnp.zeros((WIDTH, WIDTH), jnp.float32)
    first = place[0] % 2 == 0
    for n, (i, j) in enumerate(UPPER):
        a, b = mine[:, n % 3].reshape(BS, BS), other[:, n % 3].reshape(BS, BS)
        block = jnp.where(first, a, b) if n < 3 else jnp.where(first, b, a)
        work[i * BS : i * BS + BS, j * BS : j * BS + BS] = block
    inverse[...] = jnp.zeros((WIDTH, WIDTH), jnp.float32)
    eliminate(work, inverse, range(0, WIDTH // 2, FACTOR))


def corner_second(inverse_in, work_in, inverse, work):
    inverse[...] = inverse_in[...]
    work[...] = work_in[...]
    eliminate(work, inverse, range(WIDTH // 2, WIDTH, FACTOR))


CROSSED = (0, 4, 2, 6, 1, 5, 3, 7)
IN_VMEM = pl.BlockSpec(memory_space=pltpu.VMEM)
IN_SMEM = pl.BlockSpec(memory_space=pltpu.SMEM)
SQUARE = jax.ShapeDtypeStruct((WIDTH, WIDTH), jnp.float32)


def corner_half(place, mine, other):
    return pl.pallas_call(
        corner_first,
        in_specs=[IN_SMEM, IN_VMEM, IN_VMEM],
        out_specs=[IN_VMEM, IN_VMEM],
        out_shape=[SQUARE, SQUARE],
        compiler_params=pltpu.CompilerParams(vmem_limit_bytes=56 << 20),
        name="corner_first",
    )(place, mine, other)


def corner_rest(inverse, work):
    return pl.pallas_call(
        corner_second,
        in_specs=[IN_VMEM, IN_VMEM],
        out_specs=IN_VMEM,
        out_shape=SQUARE,
        scratch_shapes=[pltpu.VMEM((WIDTH, WIDTH), jnp.float32)],
        compiler_params=pltpu.CompilerParams(vmem_limit_bytes=56 << 20),
        name="corner_second",
    )(inverse, work)


def right_kernel(place, mine, other, inverse, out, lines):
    core = place[0] % 2
    z = place[0] // 2
    for k in range(PANELS):
        for n, apart in enumerate(CROSSED):
            lines[k, core, z ^ apart] = mine[n, k]
            lines[k, 1 - core, z ^ apart] = other[n, k]
    for k in range(PANELS):
        total = None
        for j in range(k + 1):
            part = full_dot(
                inverse[k * BS : k * BS + BS, j * BS : j * BS + BS],
                lines[j].reshape(BS, lines.shape[-1]),
                ((1,), (0,)),
            )
            total = part if total is None else total + part
        out[k * BS : k * BS + BS, :] = total


def right_panel(place, mine, other, inverse):
    size = mine.shape[-1]
    return pl.pallas_call(
        right_kernel,
        in_specs=[IN_SMEM] + [IN_VMEM] * 3,
        out_shape=jax.ShapeDtypeStruct((WIDTH, size), jnp.float32),
        scratch_shapes=[pltpu.VMEM((PANELS, 2, 8, 16, size), jnp.float32)],
        compiler_params=pltpu.CompilerParams(vmem_limit_bytes=56 << 20),
        name="right",
    )(place, mine, other, inverse)


def panel_kernel(place, rows, right, inverse, matrix, out, left):
    block_row = pl.program_id(0) * 16 + place[0]
    lines = [rows[:, k].reshape(BS, BS) for k in range(PANELS)]
    for k in range(PANELS):
        total = None
        for j in range(k + 1):
            part = full_dot(lines[j], inverse[k * BS : k * BS + BS, j * BS : j * BS + BS], ((1,), (1,)))
            total = part if total is None else total + part
        left[:, k * BS : k * BS + BS] = total
    out[...] = matrix[...] - full_dot(left[...], right[...], ((1,), (0,)))

    @pl.when(block_row < PANELS)
    def _():
        out[...] = jnp.zeros(out.shape, jnp.float32)

    for k in range(PANELS):

        @pl.when(place[1] == k)
        def _(k=k):
            panel = left[:, k * BS : k * BS + BS]
            r = lax.broadcasted_iota(jnp.int32, (BS, BS), 0) + block_row * BS
            s = lax.broadcasted_iota(jnp.int32, (BS, BS), 1) + k * BS
            out[:, :BS] = jnp.where(r >= s, panel, 0.0)


def panel_update(place, rows, right, inverse, matrix):
    size = matrix.shape[0]
    steps = size // BS
    pieces = rows.shape[0] // steps
    return pl.pallas_call(
        panel_kernel,
        grid_spec=pltpu.PrefetchScalarGridSpec(
            num_scalar_prefetch=1,
            grid=(steps,),
            in_specs=[
                pl.BlockSpec((pieces,) + rows.shape[1:], lambda i, _: (i, 0, 0, 0)),
                pl.BlockSpec(right.shape, lambda i, _: (0, 0)),
                pl.BlockSpec(inverse.shape, lambda i, _: (0, 0)),
                pl.BlockSpec((BS, size), lambda i, _: (i, 0)),
            ],
            out_specs=pl.BlockSpec((BS, size), lambda i, _: (i, 0)),
            scratch_shapes=[pltpu.VMEM((BS, WIDTH), jnp.float32)],
        ),
        out_shape=jax.ShapeDtypeStruct(matrix.shape, jnp.float32),
        compiler_params=pltpu.CompilerParams(vmem_limit_bytes=56 << 20),
        name="panels",
    )(place, rows, right, inverse, matrix)


def gathered(piece, axes):
    copies = jnp.broadcast_to(piece[None], (lax.axis_size(axes),) + piece.shape)
    return lax.all_to_all(copies, axes, 0, 0, tiled=True)


def swapped(piece):
    return lax.ppermute(piece, "row_1", [(0, 1), (1, 0)])


def scattered(block, z, even):
    low, high = block[: BS // 2], block[BS // 2 :]
    kept = jnp.where(even, low, high)
    came = swapped(jnp.where(even, high, low))
    first = jnp.where(even, kept, came)
    second = jnp.where(even, came, kept)
    both = jnp.stack([first, second]).reshape(2, 8, 16, -1)
    both = jnp.where(z == 1, jnp.roll(both, -1, axis=1), both)
    early, late = both[:, 0], both[0, 0]
    for s in range(1, 8):
        got = lax.ppermute(both[:, s], "row_0", [(0, s), (1, (1 + s) % 8)])
        early = jnp.where(z == s, got, early)
        late = jnp.where(z == (s + 1) % 8, got[0], late)
    return jnp.concatenate([early, late[None]])


def crossed(pieces, apart):
    got = lax.ppermute(pieces, "row_0", [(z, z ^ apart) for z in range(8)])
    return jnp.concatenate([pieces, got])


def corner_pieces(top, z, even):
    last = lax.ppermute(top[2:], ROW, [(2, 1)])
    have = jnp.where(even, top, jnp.concatenate([top[1:], last]))
    near = lax.ppermute(have, "row_0", [(0, 3)])
    far = lax.ppermute(have, "row_0", [(0, 5)])
    have = jnp.where(z == 3, near, jnp.where(z == 5, far, have))
    near = lax.ppermute(have, "row_0", [(0, 1), (3, 2), (5, 6)])
    far = lax.ppermute(have, "row_0", [(0, 7), (3, 4)])
    have = jnp.where((z == 1) | (z == 2) | (z == 6), near, have)
    return jnp.where((z == 7) | (z == 4), far, have)


def on_device(gram):
    matrix = gram[0, 0]
    place = jnp.stack([lax.axis_index(ROW), lax.axis_index(COL)]).astype(jnp.int32)
    z = lax.axis_index("row_0")
    even = lax.axis_index("row_1") == 0
    top = lax.all_to_all(matrix[:BS, :BS].reshape(16, 16, BS), COL, 0, 0, tiled=True)[:PANELS]
    below = scattered(matrix[:BS], z, even)
    top, slab = lax.optimization_barrier((top, matrix[:, :BS]))
    side = lax.all_to_all(slab.reshape(16, 64, BS), COL, 0, 0, tiled=True)[:PANELS]
    piece = corner_pieces(top, z, even)
    side, piece, below = lax.optimization_barrier((side, piece, below))
    mine = gathered(piece, COL)
    lines = crossed(below[None], 4)
    mine, lines = lax.optimization_barrier((mine, lines))
    other = swapped(mine)
    mine, other, side, lines = lax.optimization_barrier((mine, other, side, lines))
    rows = gathered(side, COL)
    lines = crossed(lines, 2)
    inverse, work = corner_half(place, mine, other)
    inverse, work, lines = lax.optimization_barrier((inverse, work, lines))
    lines = crossed(lines, 1)
    inverse = corner_rest(inverse, work)
    inverse, lines = lax.optimization_barrier((inverse, lines))
    right = right_panel(place, lines, swapped(lines), inverse)
    return panel_update(place, rows, right, inverse, matrix)[None, None]


def solution(mesh):
    split = Mesh(mesh.devices.reshape(8, 2, 4, 4), ROW + COL)
    return jax.shard_map(
        on_device,
        mesh=split,
        in_specs=(P(ROW, COL, None, None),),
        out_specs=P(ROW, COL, None, None),
        check_vma=False,
    )
```

```python
import jax
import jax.numpy as jnp
from jax import lax
from jax.experimental import pallas as pl
from jax.experimental.pallas import tpu as pltpu
from jax.sharding import Mesh
from jax.sharding import PartitionSpec as P

BS = 256
PANELS = 3
WIDTH = PANELS * BS
FACTOR = 128
ROW = ("row_0", "row_1")
COL = ("col_0", "col_1")
FULL = lax.Precision.HIGHEST
UPPER = ((0, 0), (0, 1), (0, 2), (1, 1), (1, 2), (2, 2))


def full_dot(left, right, dims):
    return lax.dot_general(
        left, right, (dims, ((), ())), precision=FULL, preferred_element_type=jnp.float32
    )


def wide(line):
    return jnp.broadcast_to(line, (8, FACTOR))


def factor_inverse(block):
    count = FACTOR // 8
    tiles = [block[8 * b : 8 * b + 8] for b in range(count)]
    lane = lax.broadcasted_iota(jnp.int32, (8, FACTOR), 1)
    sub = lax.broadcasted_iota(jnp.int32, (8, FACTOR), 0)
    for b in range(count):
        cols = {t: [wide(tiles[t][:, 8 * b + j : 8 * b + j + 1]) for j in range(8)] for t in range(b, count)}
        for s in range(8):
            at = lane == 8 * b + s
            own = cols[b]
            inv = 1.0 / wide(own[s][s : s + 1])
            heads = [wide(own[j][s : s + 1]) for j in range(8)]
            pivot = jnp.where(at, 1.0, wide(tiles[b][s : s + 1]))
            for t in range(b, count):
                scale = cols[t][s] * inv
                rest = jnp.where(at, 0.0, tiles[t])
                if t == b:
                    scale = jnp.where(sub > s, scale, 0.0)
                    rest = jnp.where(sub > s, rest, tiles[t])
                for j in range(s + 1, 8):
                    cols[t][j] = cols[t][j] - scale * heads[j]
                tiles[t] = rest - scale * pivot
    rows = []
    for b, tile in enumerate(tiles):
        own = lane == sub + 8 * b
        pivots = jnp.sum(jnp.where(own, tile, 0.0), axis=1, keepdims=True)
        scale = lax.rsqrt(pivots)
        scale = scale * (1.5 - 0.5 * pivots * scale * scale)
        rows.append(jnp.where(lane < sub + 8 * b, tile * scale, jnp.where(own, scale, 0.0)))
    return jnp.concatenate(rows, axis=0)


def corner_kernel(place, mine, other, inverse, work):
    work[...] = jnp.zeros((WIDTH, WIDTH), jnp.float32)
    first = place[0] % 2 == 0
    for n, (i, j) in enumerate(UPPER):
        a, b = mine[:, n % 3].reshape(BS, BS), other[:, n % 3].reshape(BS, BS)
        block = jnp.where(first, a, b) if n < 3 else jnp.where(first, b, a)
        work[i * BS : i * BS + BS, j * BS : j * BS + BS] = block
    for low in range(0, WIDTH, FACTOR):
        high = low + FACTOR
        own = factor_inverse(work[low:high, low:high])
        rows = full_dot(own, work[low:high, :], ((1,), (0,)))
        left = jnp.concatenate([rows[:, :low], own], axis=1) if low else own
        if high == WIDTH:
            inverse[low:high, :] = left
            break
        right = rows[:, high:]
        inverse[low:high, :] = jnp.concatenate([left, jnp.zeros_like(right)], axis=1)
        change = full_dot(right, jnp.concatenate([left, right], axis=1), ((0,), (0,)))
        if low:
            work[high:, :low] = work[high:, :low] - change[:, :low]
        work[high:, low:high] = -change[:, low:high]
        work[high:, high:] = work[high:, high:] - change[:, high:]


IN_VMEM = pl.BlockSpec(memory_space=pltpu.VMEM)
IN_SMEM = pl.BlockSpec(memory_space=pltpu.SMEM)


def corner_inverse(place, mine, other):
    return pl.pallas_call(
        corner_kernel,
        in_specs=[IN_SMEM, IN_VMEM, IN_VMEM],
        out_specs=IN_VMEM,
        out_shape=jax.ShapeDtypeStruct((WIDTH, WIDTH), jnp.float32),
        scratch_shapes=[pltpu.VMEM((WIDTH, WIDTH), jnp.float32)],
        compiler_params=pltpu.CompilerParams(vmem_limit_bytes=56 << 20),
        name="corner",
    )(place, mine, other)


def right_kernel(lines, inverse, out):
    for k in range(PANELS):
        total = None
        for j in range(k + 1):
            part = full_dot(
                inverse[k * BS : k * BS + BS, j * BS : j * BS + BS],
                lines[j * BS : j * BS + BS, :],
                ((1,), (0,)),
            )
            total = part if total is None else total + part
        out[k * BS : k * BS + BS, :] = total


def right_panel(lines, inverse):
    size = lines.shape[1]
    half = size // 2
    return pl.pallas_call(
        right_kernel,
        grid=(2,),
        in_specs=[
            pl.BlockSpec((WIDTH, half), lambda i: (0, i)),
            pl.BlockSpec((WIDTH, WIDTH), lambda i: (0, 0)),
        ],
        out_specs=pl.BlockSpec((WIDTH, half), lambda i: (0, i)),
        out_shape=jax.ShapeDtypeStruct((WIDTH, size), jnp.float32),
        compiler_params=pltpu.CompilerParams(vmem_limit_bytes=56 << 20),
        name="right",
    )(lines, inverse)


def panel_kernel(place, rows, right, inverse, matrix, out, left):
    block_row = pl.program_id(0) * 16 + place[0]
    lines = [rows[:, k, 0].reshape(BS, BS) for k in range(PANELS)]
    for k in range(PANELS):
        total = None
        for j in range(k + 1):
            part = full_dot(lines[j], inverse[k * BS : k * BS + BS, j * BS : j * BS + BS], ((1,), (1,)))
            total = part if total is None else total + part
        left[:, k * BS : k * BS + BS] = total
    out[...] = matrix[...] - full_dot(left[...], right[...], ((1,), (0,)))

    @pl.when(block_row < PANELS)
    def _():
        out[...] = jnp.zeros(out.shape, jnp.float32)

    for k in range(PANELS):

        @pl.when(place[1] == k)
        def _(k=k):
            panel = left[:, k * BS : k * BS + BS]
            r = lax.broadcasted_iota(jnp.int32, (BS, BS), 0) + block_row * BS
            s = lax.broadcasted_iota(jnp.int32, (BS, BS), 1) + k * BS
            out[:, :BS] = jnp.where(r >= s, panel, 0.0)


def panel_update(place, rows, right, inverse, matrix):
    size = matrix.shape[0]
    steps = size // BS
    return pl.pallas_call(
        panel_kernel,
        grid_spec=pltpu.PrefetchScalarGridSpec(
            num_scalar_prefetch=1,
            grid=(steps,),
            in_specs=[
                pl.BlockSpec((16, PANELS, 1, 16, BS), lambda i, _: (0, 0, i, 0, 0)),
                pl.BlockSpec(right.shape, lambda i, _: (0, 0)),
                pl.BlockSpec(inverse.shape, lambda i, _: (0, 0)),
                pl.BlockSpec((BS, size), lambda i, _: (i, 0)),
            ],
            out_specs=pl.BlockSpec((BS, size), lambda i, _: (i, 0)),
            scratch_shapes=[pltpu.VMEM((BS, WIDTH), jnp.float32)],
        ),
        out_shape=jax.ShapeDtypeStruct(matrix.shape, jnp.float32),
        compiler_params=pltpu.CompilerParams(vmem_limit_bytes=56 << 20),
        name="panels",
    )(place, rows, right, inverse, matrix)


def copies(piece):
    return jnp.broadcast_to(piece[None], (16,) + piece.shape)


def exchanged(pieces):
    return lax.all_to_all(pieces, COL, 0, 0, tiled=True)


def swapped(piece):
    return lax.ppermute(piece, "row_1", [(0, 1), (1, 0)])


def corner_pieces(top, z, even):
    last = lax.ppermute(top[2:], ROW, [(2, 1)])
    have = jnp.where(even, top, jnp.concatenate([top[1:], last]))
    near = lax.ppermute(have, "row_0", [(0, 3)])
    far = lax.ppermute(have, "row_0", [(0, 5)])
    have = jnp.where(z == 3, near, jnp.where(z == 5, far, have))
    near = lax.ppermute(have, "row_0", [(0, 1), (3, 2), (5, 6)])
    far = lax.ppermute(have, "row_0", [(0, 7), (3, 4)])
    have = jnp.where((z == 1) | (z == 2) | (z == 6), near, have)
    return jnp.where((z == 7) | (z == 4), far, have)


def on_device(gram):
    matrix = gram[0, 0]
    place = jnp.stack([lax.axis_index(ROW), lax.axis_index(COL)]).astype(jnp.int32)
    lines = lax.all_gather(matrix[:BS], ROW, axis=0, tiled=True)
    slab = matrix[:, :BS].reshape(-1, 16, 16, BS).transpose(1, 0, 2, 3)
    side = exchanged(slab)[:PANELS]
    piece = corner_pieces(side[:, 0], lax.axis_index("row_0"), lax.axis_index("row_1") == 0)
    mine = exchanged(copies(piece))
    other = swapped(mine)
    sides, mine, other = lax.optimization_barrier((copies(side), mine, other))
    rows = exchanged(sides)
    inverse = corner_inverse(place, mine, other)
    return panel_update(place, rows, right_panel(lines, inverse), inverse, matrix)[None, None]


def solution(mesh):
    split = Mesh(mesh.devices.reshape(8, 2, 4, 4), ROW + COL)
    return jax.shard_map(
        on_device,
        mesh=split,
        in_specs=(P(ROW, COL, None, None),),
        out_specs=P(ROW, COL, None, None),
        check_vma=False,
    )
```

```python
import jax
import jax.numpy as jnp
from jax import lax
from jax.experimental import pallas as pl
from jax.experimental.pallas import tpu as pltpu
from jax.sharding import Mesh
from jax.sharding import PartitionSpec as P

BS = 256
PANELS = 3
WIDTH = PANELS * BS
FACTOR = 128
ROW = ("row_0", "row_1")
COL = ("col_0", "col_1")
FULL = lax.Precision.HIGHEST
UPPER = ((0, 0), (0, 1), (0, 2), (1, 1), (1, 2), (2, 2))


def full_dot(left, right, dims):
    return lax.dot_general(
        left, right, (dims, ((), ())), precision=FULL, preferred_element_type=jnp.float32
    )


def split(value):
    high = value.astype(jnp.bfloat16)
    return high, (value - high.astype(jnp.float32)).astype(jnp.bfloat16)


def split_dot(left, right, dims):
    def one(a, b):
        return lax.dot_general(a, b, (dims, ((), ())), preferred_element_type=jnp.float32)

    return one(left[0], right[0]) + (one(left[0], right[1]) + one(left[1], right[0]))


def wide(line):
    return jnp.broadcast_to(line, (8, FACTOR))


def factor_inverse(block):
    count = FACTOR // 8
    tiles = [block[8 * b : 8 * b + 8] for b in range(count)]
    lane = lax.broadcasted_iota(jnp.int32, (8, FACTOR), 1)
    sub = lax.broadcasted_iota(jnp.int32, (8, FACTOR), 0)
    for b in range(count):
        cols = {t: [wide(tiles[t][:, 8 * b + j : 8 * b + j + 1]) for j in range(8)] for t in range(b, count)}
        for s in range(8):
            at = lane == 8 * b + s
            own = cols[b]
            inv = 1.0 / wide(own[s][s : s + 1])
            heads = [wide(own[j][s : s + 1]) for j in range(8)]
            pivot = jnp.where(at, 1.0, wide(tiles[b][s : s + 1]))
            for t in range(b, count):
                scale = cols[t][s] * inv
                rest = jnp.where(at, 0.0, tiles[t])
                for j in range(s + 1, 8):
                    cols[t][j] = cols[t][j] - scale * heads[j]
                if t == b:
                    scale = jnp.where(sub > s, scale, 0.0)
                    rest = jnp.where(sub > s, rest, tiles[t])
                tiles[t] = rest - scale * pivot
    rows = []
    for b, tile in enumerate(tiles):
        own = lane == sub + 8 * b
        pivots = jnp.sum(jnp.where(own, tile, 0.0), axis=1, keepdims=True)
        scale = lax.rsqrt(pivots)
        scale = scale * (1.5 - 0.5 * pivots * scale * scale)
        rows.append(jnp.where(lane < sub + 8 * b, tile * scale, jnp.where(own, scale, 0.0)))
    return jnp.concatenate(rows, axis=0)


def corner_kernel(place, mine, other, inverse, work):
    work[...] = jnp.zeros((WIDTH, WIDTH), jnp.float32)
    first = place[0] % 2 == 0
    for n, (i, j) in enumerate(UPPER):
        a, b = mine[:, n % 3].reshape(BS, BS), other[:, n % 3].reshape(BS, BS)
        block = jnp.where(first, a, b) if n < 3 else jnp.where(first, b, a)
        work[i * BS : i * BS + BS, j * BS : j * BS + BS] = block
    own = factor_inverse(work[:FACTOR, :FACTOR])
    for low in range(0, WIDTH, FACTOR):
        high, after = low + FACTOR, low + 2 * FACTOR
        if high < WIDTH:
            right = full_dot(own, work[low:high, high:after], ((1,), (0,)))
            following = factor_inverse(work[high:after, high:after] - full_dot(right, right, ((0,), (0,))))
        left = own
        if low:
            left = jnp.concatenate([full_dot(own, work[low:high, :low], ((1,), (0,))), own], axis=1)
        if high == WIDTH:
            inverse[low:high, :] = left
            break
        if after < WIDTH:
            right = jnp.concatenate([right, full_dot(own, work[low:high, after:], ((1,), (0,)))], axis=1)
        inverse[low:high, :] = jnp.concatenate([left, jnp.zeros_like(right)], axis=1)
        change = full_dot(right, jnp.concatenate([left, right], axis=1), ((0,), (0,)))
        if low:
            work[high:, :low] = work[high:, :low] - change[:, :low]
        work[high:, low:high] = -change[:, low:high]
        work[high:, high:] = work[high:, high:] - change[:, high:]
        own = following


IN_VMEM = pl.BlockSpec(memory_space=pltpu.VMEM)
IN_SMEM = pl.BlockSpec(memory_space=pltpu.SMEM)


def corner_inverse(place, mine, other):
    return pl.pallas_call(
        corner_kernel,
        in_specs=[IN_SMEM, IN_VMEM, IN_VMEM],
        out_specs=IN_VMEM,
        out_shape=jax.ShapeDtypeStruct((WIDTH, WIDTH), jnp.float32),
        scratch_shapes=[pltpu.VMEM((WIDTH, WIDTH), jnp.float32)],
        compiler_params=pltpu.CompilerParams(vmem_limit_bytes=56 << 20),
        name="corner",
    )(place, mine, other)


def right_kernel(lines, inverse, out_high, out_low, inverse_high, inverse_low):
    @pl.when(pl.program_id(0) == 0)
    def _():
        inverse_high[...], inverse_low[...] = split(inverse[...])

    raw = [split(lines[j * BS : j * BS + BS, :]) for j in range(PANELS)]
    for k in range(PANELS):
        at = slice(k * BS, k * BS + BS)
        total = None
        for j in range(k + 1):
            by = slice(j * BS, j * BS + BS)
            part = split_dot((inverse_high[at, by], inverse_low[at, by]), raw[j], ((1,), (0,)))
            total = part if total is None else total + part
        out_high[at, :], out_low[at, :] = split(total)


def right_panel(lines, inverse):
    size = lines.shape[1]
    half = size // 2
    part = pl.BlockSpec((WIDTH, half), lambda i: (0, i))
    whole = pl.BlockSpec((WIDTH, WIDTH), lambda i: (0, 0))
    wide_shape = jax.ShapeDtypeStruct((WIDTH, size), jnp.bfloat16)
    square = jax.ShapeDtypeStruct((WIDTH, WIDTH), jnp.bfloat16)
    return pl.pallas_call(
        right_kernel,
        grid=(2,),
        in_specs=[part, whole],
        out_specs=[part, part, whole, whole],
        out_shape=[wide_shape, wide_shape, square, square],
        compiler_params=pltpu.CompilerParams(vmem_limit_bytes=56 << 20),
        name="right",
    )(lines, inverse)


def panel_kernel(place, rows, right_high, right_low, inverse_high, inverse_low, matrix, out, left):
    block_row = pl.program_id(0) * 16 + place[0]
    raw = [split(rows[:, k, 0].reshape(BS, BS)) for k in range(PANELS)]
    change = None
    for k in range(PANELS):
        at = slice(k * BS, k * BS + BS)
        total = None
        for j in range(k + 1):
            by = slice(j * BS, j * BS + BS)
            part = split_dot(raw[j], (inverse_high[at, by], inverse_low[at, by]), ((1,), (1,)))
            total = part if total is None else total + part
        left[:, at] = total
        part = split_dot(split(total), (right_high[at, :], right_low[at, :]), ((1,), (0,)))
        change = part if change is None else change + part
    out[...] = matrix[...] - change

    @pl.when(block_row < PANELS)
    def _():
        out[...] = jnp.zeros(out.shape, jnp.float32)

    for k in range(PANELS):

        @pl.when(place[1] == k)
        def _(k=k):
            panel = left[:, k * BS : k * BS + BS]
            r = lax.broadcasted_iota(jnp.int32, (BS, BS), 0) + block_row * BS
            s = lax.broadcasted_iota(jnp.int32, (BS, BS), 1) + k * BS
            out[:, :BS] = jnp.where(r >= s, panel, 0.0)


def panel_update(place, rows, right, matrix):
    size = matrix.shape[0]
    steps = size // BS
    wide_spec = pl.BlockSpec((WIDTH, size), lambda i, _: (0, 0))
    square = pl.BlockSpec((WIDTH, WIDTH), lambda i, _: (0, 0))
    return pl.pallas_call(
        panel_kernel,
        grid_spec=pltpu.PrefetchScalarGridSpec(
            num_scalar_prefetch=1,
            grid=(steps,),
            in_specs=[
                pl.BlockSpec((16, PANELS, 1, 16, BS), lambda i, _: (0, 0, i, 0, 0)),
                wide_spec,
                wide_spec,
                square,
                square,
                pl.BlockSpec((BS, size), lambda i, _: (i, 0)),
            ],
            out_specs=pl.BlockSpec((BS, size), lambda i, _: (i, 0)),
            scratch_shapes=[pltpu.VMEM((BS, WIDTH), jnp.float32)],
        ),
        out_shape=jax.ShapeDtypeStruct(matrix.shape, jnp.float32),
        compiler_params=pltpu.CompilerParams(vmem_limit_bytes=56 << 20),
        name="panels",
    )(place, rows, *right, matrix)


def copies(piece):
    return jnp.broadcast_to(piece[None], (16,) + piece.shape)


def exchanged(pieces):
    return lax.all_to_all(pieces, COL, 0, 0, tiled=True)


def parts_kernel(matrix, slab, top, done):
    count = matrix.shape[0]
    moves = [pltpu.make_async_copy(matrix.at[0], top, done.at[count])]
    for i in range(count):
        moves.append(pltpu.make_async_copy(matrix.at[i, :, :, pl.ds(0, BS)], slab.at[:, i], done.at[i]))
    for move in moves:
        move.start()
    for move in moves:
        move.wait()


def parts(matrix):
    size = matrix.shape[0]
    count = size // BS
    in_place = pl.BlockSpec(memory_space=pl.ANY)
    return pl.pallas_call(
        parts_kernel,
        in_specs=[in_place],
        out_specs=[in_place, in_place],
        out_shape=[
            jax.ShapeDtypeStruct((16, count, 16, BS), jnp.float32),
            jax.ShapeDtypeStruct((16, 16, size), jnp.float32),
        ],
        scratch_shapes=[pltpu.SemaphoreType.DMA((count + 1,))],
        name="parts",
    )(matrix.reshape(count, 16, 16, size))


def swapped(piece):
    return lax.ppermute(piece, "row_1", [(0, 1), (1, 0)])


def corner_pieces(top, z, even):
    last = lax.ppermute(top[2:], ROW, [(2, 1)])
    have = jnp.where(even, top, jnp.concatenate([top[1:], last]))
    near = lax.ppermute(have, "row_0", [(0, 3)])
    far = lax.ppermute(have, "row_0", [(0, 5)])
    have = jnp.where(z == 3, near, jnp.where(z == 5, far, have))
    near = lax.ppermute(have, "row_0", [(0, 1), (3, 2), (5, 6)])
    far = lax.ppermute(have, "row_0", [(0, 7), (3, 4)])
    have = jnp.where((z == 1) | (z == 2) | (z == 6), near, have)
    return jnp.where((z == 7) | (z == 4), far, have)


def on_device(gram):
    matrix = gram[0, 0]
    place = jnp.stack([lax.axis_index(ROW), lax.axis_index(COL)]).astype(jnp.int32)
    slab, top = parts(matrix)
    lines = lax.all_gather(top.reshape(BS, -1), ROW, axis=0, tiled=True)
    side = exchanged(slab)[:PANELS]
    piece = corner_pieces(side[:, 0], lax.axis_index("row_0"), lax.axis_index("row_1") == 0)
    place, sides, piece = lax.optimization_barrier((place, copies(side), piece))
    mine = exchanged(copies(piece))
    sides, mine = lax.optimization_barrier((sides, mine))
    rows = exchanged(sides)
    inverse = corner_inverse(place, mine, swapped(mine))
    return panel_update(place, rows, right_panel(lines, inverse), matrix)[None, None]


def solution(mesh):
    split = Mesh(mesh.devices.reshape(8, 2, 4, 4), ROW + COL)
    return jax.shard_map(
        on_device,
        mesh=split,
        in_specs=(P(ROW, COL, None, None),),
        out_specs=P(ROW, COL, None, None),
        check_vma=False,
    )
```

```python
import jax
import jax.numpy as jnp
from jax import lax
from jax.experimental import pallas as pl
from jax.experimental.pallas import tpu as pltpu
from jax.sharding import Mesh
from jax.sharding import PartitionSpec as P

BS = 256
PANELS = 3
WIDTH = PANELS * BS
FACTOR = 128
ROW = ("row_0", "row_1")
COL = ("col_0", "col_1")
FULL = lax.Precision.HIGHEST
UPPER = ((0, 0), (0, 1), (0, 2), (1, 1), (1, 2), (2, 2))


def full_dot(left, right, dims):
    return lax.dot_general(
        left, right, (dims, ((), ())), precision=FULL, preferred_element_type=jnp.float32
    )


def split(value):
    high = value.astype(jnp.bfloat16)
    return high, (value - high.astype(jnp.float32)).astype(jnp.bfloat16)


def split_dot(left, right, dims):
    by_left, by_right = dims[0][0], dims[1][0]
    return lax.dot_general(
        jnp.concatenate([left[0], left[0], left[1]], axis=by_left),
        jnp.concatenate([right[0], right[1], right[0]], axis=by_right),
        (dims, ((), ())),
        preferred_element_type=jnp.float32,
    )


def wide(line):
    return jnp.broadcast_to(line, (8, FACTOR))


def factor_inverse(block):
    count = FACTOR // 8
    tiles = [block[8 * b : 8 * b + 8] for b in range(count)]
    lane = lax.broadcasted_iota(jnp.int32, (8, FACTOR), 1)
    sub = lax.broadcasted_iota(jnp.int32, (8, FACTOR), 0)
    for b in range(count):
        cols = {t: [wide(tiles[t][:, 8 * b + j : 8 * b + j + 1]) for j in range(8)] for t in range(b, count)}
        for s in range(8):
            at = lane == 8 * b + s
            own = cols[b]
            inv = 1.0 / wide(own[s][s : s + 1])
            heads = [wide(own[j][s : s + 1]) for j in range(8)]
            pivot = jnp.where(at, 1.0, wide(tiles[b][s : s + 1]))
            for t in range(b, count):
                scale = cols[t][s] * inv
                rest = jnp.where(at, 0.0, tiles[t])
                for j in range(s + 1, 8):
                    cols[t][j] = cols[t][j] - scale * heads[j]
                if t == b:
                    scale = jnp.where(sub > s, scale, 0.0)
                    rest = jnp.where(sub > s, rest, tiles[t])
                tiles[t] = rest - scale * pivot
    rows = []
    for b, tile in enumerate(tiles):
        own = lane == sub + 8 * b
        pivots = jnp.sum(jnp.where(own, tile, 0.0), axis=1, keepdims=True)
        scale = lax.rsqrt(pivots)
        scale = scale * (1.5 - 0.5 * pivots * scale * scale)
        rows.append(jnp.where(lane < sub + 8 * b, tile * scale, jnp.where(own, scale, 0.0)))
    return jnp.concatenate(rows, axis=0)


def corner_kernel(place, mine, other, inverse_high, inverse_low, work):
    work[...] = jnp.zeros((WIDTH, WIDTH), jnp.float32)
    first = place[0] % 2 == 0
    for n, (i, j) in enumerate(UPPER):
        a, b = mine[:, n % 3].reshape(BS, BS), other[:, n % 3].reshape(BS, BS)
        block = jnp.where(first, a, b) if n < 3 else jnp.where(first, b, a)
        work[i * BS : i * BS + BS, j * BS : j * BS + BS] = block
    own = factor_inverse(work[:FACTOR, :FACTOR])
    for low in range(0, WIDTH, FACTOR):
        high, after = low + FACTOR, low + 2 * FACTOR
        if high < WIDTH:
            right = full_dot(own, work[low:high, high:after], ((1,), (0,)))
            following = factor_inverse(work[high:after, high:after] - full_dot(right, right, ((0,), (0,))))
        left = own
        if low:
            left = jnp.concatenate([full_dot(own, work[low:high, :low], ((1,), (0,))), own], axis=1)
        if high == WIDTH:
            inverse_high[low:high, :], inverse_low[low:high, :] = split(left)
            break
        if after < WIDTH:
            right = jnp.concatenate([right, full_dot(own, work[low:high, after:], ((1,), (0,)))], axis=1)
        lines = jnp.concatenate([left, jnp.zeros_like(right)], axis=1)
        inverse_high[low:high, :], inverse_low[low:high, :] = split(lines)
        change = full_dot(right, jnp.concatenate([left, right], axis=1), ((0,), (0,)))
        if low:
            work[high:, :low] = work[high:, :low] - change[:, :low]
        work[high:, low:high] = -change[:, low:high]
        work[high:, high:] = work[high:, high:] - change[:, high:]
        own = following


IN_VMEM = pl.BlockSpec(memory_space=pltpu.VMEM)
IN_SMEM = pl.BlockSpec(memory_space=pltpu.SMEM)


def corner_inverse(place, mine, other):
    return pl.pallas_call(
        corner_kernel,
        in_specs=[IN_SMEM, IN_VMEM, IN_VMEM],
        out_specs=[IN_VMEM, IN_VMEM],
        out_shape=[jax.ShapeDtypeStruct((WIDTH, WIDTH), jnp.bfloat16)] * 2,
        scratch_shapes=[pltpu.VMEM((WIDTH, WIDTH), jnp.float32)],
        compiler_params=pltpu.CompilerParams(vmem_limit_bytes=56 << 20),
        name="corner",
    )(place, mine, other)


def panel_kernel(
    place, lines, inverse_high, inverse_low, rows, matrix, out,
    raw_high, raw_low, known_high, known_low, right_high, right_low, left, high, low,
):
    step = pl.program_id(0)

    for k in range(PANELS):
        at, end = slice(k * BS, k * BS + BS), k * BS + BS

        @pl.when(step == k)
        def _(at=at, end=end):
            raw_high[at, :], raw_low[at, :] = split(lines[...])
            known_high[at, :], known_low[at, :] = inverse_high[...], inverse_low[...]
            known = inverse_high[:, :end], inverse_low[:, :end]
            total = split_dot(known, (raw_high[:end, :], raw_low[:end, :]), ((1,), (0,)))
            right_high[at, :], right_low[at, :] = split(total)

    block_row = (step - PANELS) * 16 + place[0]

    @pl.when(step >= PANELS)
    def _():
        for k in range(PANELS):
            at = slice(k * BS, k * BS + BS)
            high[:, at], low[:, at] = split(rows[:, k, 0].reshape(BS, BS))
        for k in range(PANELS):
            at, end = slice(k * BS, k * BS + BS), k * BS + BS
            known = known_high[at, :end], known_low[at, :end]
            left[:, at] = split_dot((high[:, :end], low[:, :end]), known, ((1,), (1,)))
        change = split_dot(split(left[...]), (right_high[...], right_low[...]), ((1,), (0,)))
        out[...] = matrix[...] - change

    @pl.when((step >= PANELS) & (block_row < PANELS))
    def _():
        out[...] = jnp.zeros(out.shape, jnp.float32)

    for k in range(PANELS):

        @pl.when((step >= PANELS) & (place[1] == k))
        def _(k=k):
            panel = left[:, k * BS : k * BS + BS]
            r = lax.broadcasted_iota(jnp.int32, (BS, BS), 0) + block_row * BS
            s = lax.broadcasted_iota(jnp.int32, (BS, BS), 1) + k * BS
            out[:, :BS] = jnp.where(r >= s, panel, 0.0)


def panel_update(place, lines, inverse, rows, matrix):
    size = matrix.shape[0]

    def panel(i, _):
        return jnp.minimum(i, PANELS - 1), 0

    def block(i, _):
        return jnp.maximum(i - PANELS, 0), 0

    narrow = pltpu.VMEM((BS, WIDTH), jnp.bfloat16)
    square = pltpu.VMEM((WIDTH, WIDTH), jnp.bfloat16)
    whole = pltpu.VMEM((WIDTH, size), jnp.bfloat16)
    return pl.pallas_call(
        panel_kernel,
        grid_spec=pltpu.PrefetchScalarGridSpec(
            num_scalar_prefetch=1,
            grid=(PANELS + size // BS,),
            in_specs=[
                pl.BlockSpec((BS, size), panel),
                pl.BlockSpec((BS, WIDTH), panel),
                pl.BlockSpec((BS, WIDTH), panel),
                pl.BlockSpec((16, PANELS, 1, 16, BS), lambda i, _: (0, 0, jnp.maximum(i - PANELS, 0), 0, 0)),
                pl.BlockSpec((BS, size), block),
            ],
            out_specs=pl.BlockSpec((BS, size), block),
            scratch_shapes=[
                whole, whole, square, square, whole, whole,
                pltpu.VMEM((BS, WIDTH), jnp.float32), narrow, narrow,
            ],
        ),
        out_shape=jax.ShapeDtypeStruct(matrix.shape, jnp.float32),
        compiler_params=pltpu.CompilerParams(vmem_limit_bytes=56 << 20),
        name="panels",
    )(place, lines, *inverse, rows, matrix)


def copies(piece):
    return jnp.broadcast_to(piece[None], (16,) + piece.shape)


def exchanged(pieces):
    return lax.all_to_all(pieces, COL, 0, 0, tiled=True)


def swapped(piece):
    return lax.ppermute(piece, "row_1", [(0, 1), (1, 0)])


def corner_pieces(top, z, even):
    last = lax.ppermute(top[2:], ROW, [(2, 1)])
    have = jnp.where(even, top, jnp.concatenate([top[1:], last]))
    near = lax.ppermute(have, "row_0", [(0, 3)])
    far = lax.ppermute(have, "row_0", [(0, 5)])
    have = jnp.where(z == 3, near, jnp.where(z == 5, far, have))
    near = lax.ppermute(have, "row_0", [(0, 1), (3, 2), (5, 6)])
    far = lax.ppermute(have, "row_0", [(0, 7), (3, 4)])
    have = jnp.where((z == 1) | (z == 2) | (z == 6), near, have)
    return jnp.where((z == 7) | (z == 4), far, have)


def on_device(gram):
    matrix = gram[0, 0]
    place = jnp.stack([lax.axis_index(ROW), lax.axis_index(COL)]).astype(jnp.int32)
    slab = matrix[:, :BS].reshape(-1, 16, 16, BS).transpose(1, 0, 2, 3)
    slab, top = lax.optimization_barrier((slab, matrix))
    lines = lax.all_gather(top[:BS], ROW, axis=0, tiled=True)
    side = exchanged(slab)[:PANELS]
    piece = corner_pieces(side[:, 0], lax.axis_index("row_0"), lax.axis_index("row_1") == 0)
    place, sides, piece = lax.optimization_barrier((place, copies(side), piece))
    mine = exchanged(copies(piece))
    sides, mine = lax.optimization_barrier((sides, mine))
    rows = exchanged(sides)
    inverse = corner_inverse(place, mine, swapped(mine))
    return panel_update(place, lines, inverse, rows, matrix)[None, None]


def solution(mesh):
    split = Mesh(mesh.devices.reshape(8, 2, 4, 4), ROW + COL)
    return jax.shard_map(
        on_device,
        mesh=split,
        in_specs=(P(ROW, COL, None, None),),
        out_specs=P(ROW, COL, None, None),
        check_vma=False,
    )
```

```python
import jax
import jax.numpy as jnp
from jax import lax
from jax.experimental import pallas as pl
from jax.experimental.pallas import tpu as pltpu
from jax.sharding import Mesh
from jax.sharding import PartitionSpec as P

BS = 256
PANELS = 3
WIDTH = PANELS * BS
FACTOR = 128
ROW = ("row_0", "row_1")
COL = ("col_0", "col_1")
FULL = lax.Precision.HIGHEST
UPPER = ((0, 0), (0, 1), (0, 2), (1, 1), (1, 2), (2, 2))


def full_dot(left, right, dims):
    return lax.dot_general(
        left, right, (dims, ((), ())), precision=FULL, preferred_element_type=jnp.float32
    )


def split(value):
    high = value.astype(jnp.bfloat16)
    return high, (value - high.astype(jnp.float32)).astype(jnp.bfloat16)


DEEP = 3 * BS


def store_hhl(ref, rows, cols, value, axis):
    high, low = split(value)
    store_deep(ref, rows, cols, (high, high, low), axis)


def store_hlh(ref, rows, cols, value, axis):
    high, low = split(value)
    store_deep(ref, rows, cols, (high, low, high), axis)


def store_deep(ref, rows, cols, parts, axis):
    for n, part in enumerate(parts):
        if axis == 0:
            ref[rows * DEEP + n * BS : rows * DEEP + n * BS + BS, :] = part
        else:
            ref[rows * BS : rows * BS + BS, cols * DEEP + n * BS : cols * DEEP + n * BS + BS] = part


def deep_dot(left, right, dims):
    return lax.dot_general(left, right, (dims, ((), ())), preferred_element_type=jnp.float32)


def wide(line):
    return jnp.broadcast_to(line, (8, FACTOR))


def factor_inverse(block):
    count = FACTOR // 8
    tiles = [block[8 * b : 8 * b + 8] for b in range(count)]
    lane = lax.broadcasted_iota(jnp.int32, (8, FACTOR), 1)
    sub = lax.broadcasted_iota(jnp.int32, (8, FACTOR), 0)
    for b in range(count):
        cols = {t: [wide(tiles[t][:, 8 * b + j : 8 * b + j + 1]) for j in range(8)] for t in range(b, count)}
        for s in range(8):
            at = lane == 8 * b + s
            own = cols[b]
            inv = 1.0 / wide(own[s][s : s + 1])
            heads = [wide(own[j][s : s + 1]) for j in range(8)]
            pivot = jnp.where(at, 1.0, wide(tiles[b][s : s + 1]))
            for t in range(b, count):
                scale = cols[t][s] * inv
                rest = jnp.where(at, 0.0, tiles[t])
                for j in range(s + 1, 8):
                    cols[t][j] = cols[t][j] - scale * heads[j]
                if t == b:
                    scale = jnp.where(sub > s, scale, 0.0)
                    rest = jnp.where(sub > s, rest, tiles[t])
                tiles[t] = rest - scale * pivot
    rows = []
    for b, tile in enumerate(tiles):
        own = lane == sub + 8 * b
        pivots = jnp.sum(jnp.where(own, tile, 0.0), axis=1, keepdims=True)
        scale = lax.rsqrt(pivots)
        scale = scale * (1.5 - 0.5 * pivots * scale * scale)
        rows.append(jnp.where(lane < sub + 8 * b, tile * scale, jnp.where(own, scale, 0.0)))
    return jnp.concatenate(rows, axis=0)


def corner_kernel(place, mine, other, inverse_high, inverse_low, work):
    first = place[0] % 2 == 0
    for n, (i, j) in enumerate(UPPER):
        a, b = mine[:, n % 3].reshape(BS, BS), other[:, n % 3].reshape(BS, BS)
        block = jnp.where(first, a, b) if n < 3 else jnp.where(first, b, a)
        work[i * BS : i * BS + BS, j * BS : j * BS + BS] = block
    own = factor_inverse(work[:FACTOR, :FACTOR])
    for low in range(0, WIDTH, FACTOR):
        high, after = low + FACTOR, low + 2 * FACTOR
        if high < WIDTH:
            right = full_dot(own, work[low:high, high:after], ((1,), (0,)))
            following = factor_inverse(work[high:after, high:after] - full_dot(right, right, ((0,), (0,))))
        left = own
        if low:
            left = jnp.concatenate([full_dot(own, work[low:high, :low], ((1,), (0,))), own], axis=1)
        if high == WIDTH:
            inverse_high[low:high, :], inverse_low[low:high, :] = split(left)
            break
        if after < WIDTH:
            right = jnp.concatenate([right, full_dot(own, work[low:high, after:], ((1,), (0,)))], axis=1)
        lines = jnp.concatenate([left, jnp.zeros_like(right)], axis=1)
        inverse_high[low:high, :], inverse_low[low:high, :] = split(lines)
        change = full_dot(right, jnp.concatenate([left, right], axis=1), ((0,), (0,)))
        if low:
            work[high:, :low] = work[high:, :low] - change[:, :low]
        work[high:, low:high] = -change[:, low:high]
        work[high:, high:] = work[high:, high:] - change[:, high:]
        own = following


IN_VMEM = pl.BlockSpec(memory_space=pltpu.VMEM)
IN_SMEM = pl.BlockSpec(memory_space=pltpu.SMEM)


def corner_inverse(place, mine, other):
    return pl.pallas_call(
        corner_kernel,
        in_specs=[IN_SMEM, IN_VMEM, IN_VMEM],
        out_specs=[IN_VMEM, IN_VMEM],
        out_shape=[jax.ShapeDtypeStruct((WIDTH, WIDTH), jnp.bfloat16)] * 2,
        scratch_shapes=[pltpu.VMEM((WIDTH, WIDTH), jnp.float32)],
        compiler_params=pltpu.CompilerParams(vmem_limit_bytes=56 << 20),
        name="corner",
    )(place, mine, other)


def panel_kernel(place, lines, inverse_high, inverse_low, rows, matrix, out, raw, known, right, left, side, change):
    step = pl.program_id(0)

    for k in range(PANELS):

        @pl.when(step == k)
        def _(k=k):
            end = DEEP * (k + 1)
            store_hhl(raw, k, 0, lines[...], 0)
            for j in range(k + 1):
                high, low = inverse_high[:, j * BS : j * BS + BS], inverse_low[:, j * BS : j * BS + BS]
                store_deep(known, k, j, (high, low, high), 1)
            total = deep_dot(known[k * BS : k * BS + BS, :end], raw[:end, :], ((1,), (0,)))
            store_hlh(right, k, 0, total, 0)

    block_row = (step - PANELS) * 16 + place[0]

    @pl.when(step >= PANELS)
    def _():
        for k in range(PANELS):
            store_hhl(side, 0, k, rows[:, k, 0].reshape(BS, BS), 1)
        for k in range(PANELS):
            at, end = slice(k * BS, k * BS + BS), DEEP * (k + 1)
            total = deep_dot(side[:, :end], known[at, :end], ((1,), (1,)))
            left[:, at] = total
            store_hhl(change, 0, k, total, 1)
        out[...] = matrix[...] - deep_dot(change[...], right[...], ((1,), (0,)))

    @pl.when((step >= PANELS) & (block_row < PANELS))
    def _():
        out[...] = jnp.zeros(out.shape, jnp.float32)

    for k in range(PANELS):

        @pl.when((step >= PANELS) & (place[1] == k))
        def _(k=k):
            panel = left[:, k * BS : k * BS + BS]
            r = lax.broadcasted_iota(jnp.int32, (BS, BS), 0) + block_row * BS
            s = lax.broadcasted_iota(jnp.int32, (BS, BS), 1) + k * BS
            out[:, :BS] = jnp.where(r >= s, panel, 0.0)


def panel_update(place, lines, inverse, rows, matrix):
    size = matrix.shape[0]

    def panel(i, _):
        return jnp.minimum(i, PANELS - 1), 0

    def block(i, _):
        return jnp.maximum(i - PANELS, 0), 0

    deep = 3 * WIDTH
    return pl.pallas_call(
        panel_kernel,
        grid_spec=pltpu.PrefetchScalarGridSpec(
            num_scalar_prefetch=1,
            grid=(PANELS + size // BS,),
            in_specs=[
                pl.BlockSpec((BS, size), panel),
                pl.BlockSpec((BS, WIDTH), panel),
                pl.BlockSpec((BS, WIDTH), panel),
                pl.BlockSpec((16, PANELS, 1, 16, BS), lambda i, _: (0, 0, jnp.maximum(i - PANELS, 0), 0, 0)),
                pl.BlockSpec((BS, size), block),
            ],
            out_specs=pl.BlockSpec((BS, size), block),
            scratch_shapes=[
                pltpu.VMEM((deep, size), jnp.bfloat16),
                pltpu.VMEM((WIDTH, deep), jnp.bfloat16),
                pltpu.VMEM((deep, size), jnp.bfloat16),
                pltpu.VMEM((BS, WIDTH), jnp.float32),
                pltpu.VMEM((BS, deep), jnp.bfloat16),
                pltpu.VMEM((BS, deep), jnp.bfloat16),
            ],
        ),
        out_shape=jax.ShapeDtypeStruct(matrix.shape, jnp.float32),
        compiler_params=pltpu.CompilerParams(vmem_limit_bytes=56 << 20),
        name="panels",
    )(place, lines, *inverse, rows, matrix)


def copies(piece):
    return jnp.broadcast_to(piece[None], (16,) + piece.shape)


def exchanged(pieces):
    return lax.all_to_all(pieces, COL, 0, 0, tiled=True)


def swapped(piece):
    return lax.ppermute(piece, "row_1", [(0, 1), (1, 0)])


def corner_pieces(top, z, even):
    last = lax.ppermute(top[2:], ROW, [(2, 1)])
    have = jnp.where(even, top, jnp.concatenate([top[1:], last]))
    near = lax.ppermute(have, "row_0", [(0, 3)])
    far = lax.ppermute(have, "row_0", [(0, 5)])
    have = jnp.where(z == 3, near, jnp.where(z == 5, far, have))
    near = lax.ppermute(have, "row_0", [(0, 1), (3, 2), (5, 6)])
    far = lax.ppermute(have, "row_0", [(0, 7), (3, 4)])
    have = jnp.where((z == 1) | (z == 2) | (z == 6), near, have)
    return jnp.where((z == 7) | (z == 4), far, have)


def on_device(gram):
    matrix = gram[0, 0]
    place = jnp.stack([lax.axis_index(ROW), lax.axis_index(COL)]).astype(jnp.int32)
    top, below = lax.optimization_barrier((matrix[:BS], matrix))
    lines = lax.all_gather(top, ROW, axis=0, tiled=True)
    slab = below[:, :BS].reshape(-1, 16, 16, BS).transpose(1, 0, 2, 3)
    side = exchanged(slab)[:PANELS]
    piece = corner_pieces(side[:, 0], lax.axis_index("row_0"), lax.axis_index("row_1") == 0)
    mine = exchanged(copies(piece))
    place, sides, mine = lax.optimization_barrier((place, copies(side), mine))
    rows = exchanged(sides)
    inverse = corner_inverse(place, mine, swapped(mine))
    return panel_update(place, lines, inverse, rows, matrix)[None, None]


def solution(mesh):
    split = Mesh(mesh.devices.reshape(8, 2, 4, 4), ROW + COL)
    return jax.shard_map(
        on_device,
        mesh=split,
        in_specs=(P(ROW, COL, None, None),),
        out_specs=P(ROW, COL, None, None),
        check_vma=False,
    )
```

```python
import jax
import jax.numpy as jnp
from jax import lax
from jax.experimental import pallas as pl
from jax.experimental.pallas import tpu as pltpu
from jax.sharding import Mesh
from jax.sharding import PartitionSpec as P

BS = 256
PANELS = 3
WIDTH = PANELS * BS
FACTOR = 128
ROW = ("row_0", "row_1")
COL = ("col_0", "col_1")
FULL = lax.Precision.HIGHEST
UPPER = ((0, 0), (0, 1), (0, 2), (1, 1), (1, 2), (2, 2))


def full_dot(left, right, dims):
    return lax.dot_general(
        left, right, (dims, ((), ())), precision=FULL, preferred_element_type=jnp.float32
    )


def split(value):
    high = value.astype(jnp.bfloat16)
    return high, (value - high.astype(jnp.float32)).astype(jnp.bfloat16)


def split_dot(left, right, dims):
    by_left, by_right = dims[0][0], dims[1][0]
    return lax.dot_general(
        jnp.concatenate([left[0], left[0], left[1]], axis=by_left),
        jnp.concatenate([right[0], right[1], right[0]], axis=by_right),
        (dims, ((), ())),
        preferred_element_type=jnp.float32,
    )


def wide(line):
    return jnp.broadcast_to(line, (8, FACTOR))


def factor_inverse(block):
    count = FACTOR // 8
    tiles = [block[8 * b : 8 * b + 8] for b in range(count)]
    lane = lax.broadcasted_iota(jnp.int32, (8, FACTOR), 1)
    sub = lax.broadcasted_iota(jnp.int32, (8, FACTOR), 0)
    for b in range(count):
        cols = {t: [wide(tiles[t][:, 8 * b + j : 8 * b + j + 1]) for j in range(8)] for t in range(b, count)}
        for s in range(8):
            at = lane == 8 * b + s
            own = cols[b]
            inv = 1.0 / wide(own[s][s : s + 1])
            heads = [wide(own[j][s : s + 1]) for j in range(8)]
            pivot = jnp.where(at, 1.0, wide(tiles[b][s : s + 1]))
            for t in range(b, count):
                scale = cols[t][s] * inv
                rest = jnp.where(at, 0.0, tiles[t])
                for j in range(s + 1, 8):
                    cols[t][j] = cols[t][j] - scale * heads[j]
                if t == b:
                    scale = jnp.where(sub > s, scale, 0.0)
                    rest = jnp.where(sub > s, rest, tiles[t])
                tiles[t] = rest - scale * pivot
    rows = []
    for b, tile in enumerate(tiles):
        own = lane == sub + 8 * b
        pivots = jnp.sum(jnp.where(own, tile, 0.0), axis=1, keepdims=True)
        scale = lax.rsqrt(pivots)
        scale = scale * (1.5 - 0.5 * pivots * scale * scale)
        rows.append(jnp.where(lane < sub + 8 * b, tile * scale, jnp.where(own, scale, 0.0)))
    return jnp.concatenate(rows, axis=0)


def corner_kernel(place, mine, other, inverse_high, inverse_low, work):
    work[...] = jnp.zeros((WIDTH, WIDTH), jnp.float32)
    first = place[0] % 2 == 0
    for n, (i, j) in enumerate(UPPER):
        a, b = mine[:, n % 3].reshape(BS, BS), other[:, n % 3].reshape(BS, BS)
        block = jnp.where(first, a, b) if n < 3 else jnp.where(first, b, a)
        work[i * BS : i * BS + BS, j * BS : j * BS + BS] = block
    own = factor_inverse(work[:FACTOR, :FACTOR])
    for low in range(0, WIDTH, FACTOR):
        high, after = low + FACTOR, low + 2 * FACTOR
        if high < WIDTH:
            right = full_dot(own, work[low:high, high:after], ((1,), (0,)))
            following = factor_inverse(work[high:after, high:after] - full_dot(right, right, ((0,), (0,))))
        left = own
        if low:
            left = jnp.concatenate([full_dot(own, work[low:high, :low], ((1,), (0,))), own], axis=1)
        if high == WIDTH:
            inverse_high[low:high, :], inverse_low[low:high, :] = split(left)
            break
        if after < WIDTH:
            right = jnp.concatenate([right, full_dot(own, work[low:high, after:], ((1,), (0,)))], axis=1)
        lines = jnp.concatenate([left, jnp.zeros_like(right)], axis=1)
        inverse_high[low:high, :], inverse_low[low:high, :] = split(lines)
        change = full_dot(right, jnp.concatenate([left, right], axis=1), ((0,), (0,)))
        if low:
            work[high:, :low] = work[high:, :low] - change[:, :low]
        work[high:, low:high] = -change[:, low:high]
        work[high:, high:] = work[high:, high:] - change[:, high:]
        own = following


IN_VMEM = pl.BlockSpec(memory_space=pltpu.VMEM)
IN_SMEM = pl.BlockSpec(memory_space=pltpu.SMEM)


def corner_inverse(place, mine, other):
    return pl.pallas_call(
        corner_kernel,
        in_specs=[IN_SMEM, IN_VMEM, IN_VMEM],
        out_specs=[IN_VMEM, IN_VMEM],
        out_shape=[jax.ShapeDtypeStruct((WIDTH, WIDTH), jnp.bfloat16)] * 2,
        scratch_shapes=[pltpu.VMEM((WIDTH, WIDTH), jnp.float32)],
        compiler_params=pltpu.CompilerParams(vmem_limit_bytes=56 << 20),
        name="corner",
    )(place, mine, other)


def panel_kernel(
    place, lines, inverse_high, inverse_low, rows, matrix, out,
    raw_high, raw_low, known_high, known_low, right_high, right_low, left, high, low,
):
    step = pl.program_id(0)

    for k in range(PANELS):
        at, end = slice(k * BS, k * BS + BS), k * BS + BS

        @pl.when(step == k)
        def _(at=at, end=end):
            raw_high[at, :], raw_low[at, :] = split(lines[...])
            known_high[at, :], known_low[at, :] = inverse_high[...], inverse_low[...]
            known = inverse_high[:, :end], inverse_low[:, :end]
            total = split_dot(known, (raw_high[:end, :], raw_low[:end, :]), ((1,), (0,)))
            right_high[at, :], right_low[at, :] = split(total)

    block_row = (step - PANELS) * 16 + place[0]

    @pl.when(step >= PANELS)
    def _():
        for k in range(PANELS):
            at = slice(k * BS, k * BS + BS)
            high[:, at], low[:, at] = split(rows[:, k, 0].reshape(BS, BS))
        for k in range(PANELS):
            at, end = slice(k * BS, k * BS + BS), k * BS + BS
            known = known_high[at, :end], known_low[at, :end]
            left[:, at] = split_dot((high[:, :end], low[:, :end]), known, ((1,), (1,)))
        change = split_dot(split(left[...]), (right_high[...], right_low[...]), ((1,), (0,)))
        out[...] = matrix[...] - change

    @pl.when((step >= PANELS) & (block_row < PANELS))
    def _():
        out[...] = jnp.zeros(out.shape, jnp.float32)

    for k in range(PANELS):

        @pl.when((step >= PANELS) & (place[1] == k))
        def _(k=k):
            panel = left[:, k * BS : k * BS + BS]
            r = lax.broadcasted_iota(jnp.int32, (BS, BS), 0) + block_row * BS
            s = lax.broadcasted_iota(jnp.int32, (BS, BS), 1) + k * BS
            out[:, :BS] = jnp.where(r >= s, panel, 0.0)


def panel_update(place, lines, inverse, rows, matrix):
    size = matrix.shape[0]

    def panel(i, _):
        return jnp.minimum(i, PANELS - 1), 0

    def block(i, _):
        return jnp.maximum(i - PANELS, 0), 0

    narrow = pltpu.VMEM((BS, WIDTH), jnp.bfloat16)
    square = pltpu.VMEM((WIDTH, WIDTH), jnp.bfloat16)
    whole = pltpu.VMEM((WIDTH, size), jnp.bfloat16)
    return pl.pallas_call(
        panel_kernel,
        grid_spec=pltpu.PrefetchScalarGridSpec(
            num_scalar_prefetch=1,
            grid=(PANELS + size // BS,),
            in_specs=[
                pl.BlockSpec((BS, size), panel),
                pl.BlockSpec((BS, WIDTH), panel),
                pl.BlockSpec((BS, WIDTH), panel),
                pl.BlockSpec((16, PANELS, 1, 16, BS), lambda i, _: (0, 0, jnp.maximum(i - PANELS, 0), 0, 0)),
                pl.BlockSpec((BS, size), block),
            ],
            out_specs=pl.BlockSpec((BS, size), block),
            scratch_shapes=[
                whole, whole, square, square, whole, whole,
                pltpu.VMEM((BS, WIDTH), jnp.float32), narrow, narrow,
            ],
        ),
        out_shape=jax.ShapeDtypeStruct(matrix.shape, jnp.float32),
        compiler_params=pltpu.CompilerParams(vmem_limit_bytes=56 << 20),
        name="panels",
    )(place, lines, *inverse, rows, matrix)


def copies(piece):
    return jnp.broadcast_to(piece[None], (16,) + piece.shape)


def exchanged(pieces):
    return lax.all_to_all(pieces, COL, 0, 0, tiled=True)


def swapped(piece):
    return lax.ppermute(piece, "row_1", [(0, 1), (1, 0)])


def corner_pieces(top, z, even):
    have = jnp.where(even, top, jnp.concatenate([top[1:], top[2:]]))
    near = lax.ppermute(have, "row_0", [(0, 3)])
    far = lax.ppermute(have, "row_0", [(0, 5)])
    last = [lax.ppermute(top[2:], ROW, [(2, 2 * at + 1)]) for at in (0, 3, 5)]
    have = jnp.where(z == 3, near, jnp.where(z == 5, far, have))
    last = jnp.where(z == 3, last[1], jnp.where(z == 5, last[2], last[0]))
    have = jnp.concatenate([have[:2], jnp.where(even, have[2:], last)])
    near = lax.ppermute(have, "row_0", [(0, 1), (3, 2), (5, 6)])
    far = lax.ppermute(have, "row_0", [(0, 7), (3, 4)])
    have = jnp.where((z == 1) | (z == 2) | (z == 6), near, have)
    return jnp.where((z == 7) | (z == 4), far, have)


def on_device(gram):
    matrix = gram[0, 0]
    place = jnp.stack([lax.axis_index(ROW), lax.axis_index(COL)]).astype(jnp.int32)
    top, below = lax.optimization_barrier((matrix[:BS], matrix))
    lines = lax.all_gather(top, ROW, axis=0, tiled=True)
    slab = below[:, :BS].reshape(-1, 16, 16, BS).transpose(1, 0, 2, 3)
    side = exchanged(slab)[:PANELS]
    piece = corner_pieces(side[:, 0], lax.axis_index("row_0"), lax.axis_index("row_1") == 0)
    place, sides, piece = lax.optimization_barrier((place, copies(side), piece))
    mine = exchanged(copies(piece))
    other = swapped(mine)
    sides, mine, other = lax.optimization_barrier((sides, mine, other))
    rows = exchanged(sides)
    inverse = corner_inverse(place, mine, other)
    return panel_update(place, lines, inverse, rows, matrix)[None, None]


def solution(mesh):
    split = Mesh(mesh.devices.reshape(8, 2, 4, 4), ROW + COL)
    return jax.shard_map(
        on_device,
        mesh=split,
        in_specs=(P(ROW, COL, None, None),),
        out_specs=P(ROW, COL, None, None),
        check_vma=False,
    )
```
